128 devices in a mesh: head: 4 (over x), seq: 32 (over z, y, core).
Axes of the slice: x: 4, y: 4, z: 4, core: 2. Of those that a mesh axis runs over, the one named last changes fastest.
Arguments:
- q_nope: bfloat16 [4096, 16384], P('seq', 'head'), may hold values from -6 to 6
- q_rope: bfloat16 [4096, 8192], P('seq', 'head'), may hold values from -128 to 128
- kv_latent: bfloat16 [4096, 576], P('seq'), may hold values from -10 to 10
- group_ids: int32 [4096], replicated, may hold values from 0 to 63, never falling along the last dimension, each value on 1 to 128 neighbouring positions
- w_uk: bfloat16 [128, 128, 512], P('head'), may hold values from -0.5 to 0.5
- w_uv: bfloat16 [128, 512, 128], P('head'), may hold values from -0.25 to 0.25
- moe_in: bfloat16 [8192, 7168], P('seq', 'head'), may hold values from -6 to 6
- expert_ids: int32 [8192, 2], P('seq'), may hold values from 0 to 31, all different within a row; in each aligned block of 256 rows (0 to 255, 256 to 511, ...) at most 32 rows name the same one
- gate_w: float32 [8192, 2], P('seq'), may hold values from 0.1 to 1
- w_gate: bfloat16 [32, 7168, 1024], P('seq', 'head'), may hold values from -0.0625 to 0.0625
- w_up: bfloat16 [32, 7168, 1024], P('seq', 'head'), may hold values from -0.0625 to 0.0625
- w_down: bfloat16 [32, 1024, 7168], P('seq', None, 'head'), may hold values from -0.1875 to 0.1875
Outputs:
- attn_out: bfloat16 [4096, 16384], P('seq', 'head')
- moe_out: bfloat16 [8192, 7168], P('seq', 'head')
The draws below stay inside these ranges and needn't reach their ends.
Inputs may be any that keep to these rules, and one draw needn't show every extreme that they name: `expert_ids`: each row names 2 different experts. Among the routes of one aligned block of 256 rows (the rows of one index of seq) no expert is named more than 32 times, a bound that some block reaches. `group_ids`: never falls along the rows; each group holds 1 to 128 consecutive tokens, one exactly 128.
All inputs are finite; a program needn't handle non-finite values.
Results may differ from the reference program's by a relative error of at most 0.007.
Values may be sent and summed in bfloat16 or wider, within the bound.
No kernel may reach another device: no remote copies, remote signals or barrier semaphores. Data moves between devices by JAX's collectives and lax.ppermute only.
A program may use at most 192 MiB of HBM per device.

```python
import math
import jax
import jax.numpy as jnp
import numpy as np
from jax import lax

D = 7168
HEADS = 128
NOPE = 128
ROPE = 64
LAT = 512
VDIM = 128
FF = 1024
TOPW = 2
ATT_TOK = 128
MOE_TOK = 256
EXPERTS = 32
CAP = 32
ATT_ROWS = 4096
MOE_ROWS = 8192
GROUPS = 64
N_SEQ = 32


def draw_kv_latent(key, part):
    latent = jnp.clip(jax.random.normal(jax.random.fold_in(key, 11), (ATT_ROWS, LAT), jnp.float32), -6.0, 6.0)
    rotary = jnp.clip(jax.random.normal(jax.random.fold_in(key, 13), (ATT_ROWS, ROPE), jnp.float32), -6.0, 6.0)
    return jnp.concatenate([latent, rotary], axis=1).astype(jnp.bfloat16)


def draw_q_rope(key, part):
    noise = jax.random.normal(jax.random.fold_in(key, 17), (ATT_ROWS // 8, 8, HEADS, ROPE), jnp.float32)
    noise = jnp.clip(noise, -6.0, 6.0)
    values = noise
    return values.reshape(ATT_ROWS, HEADS * ROPE).astype(jnp.bfloat16)


def shard_levels(key, shape, split, least, high):
    loudness = 1.0
    for axis_at, parts in split:
        heights = jax.random.uniform(jax.random.fold_in(jax.random.fold_in(key, 6), axis_at), (parts,), jnp.float32, least / len(split), high / len(split))
        loudness = loudness * jnp.repeat(jnp.exp(heights), shape[axis_at] // parts).reshape((-1,) + (1,) * (len(shape) - 1 - axis_at))
    return loudness


def split_up(number_of, total, reach, slope):
    weights = [(1 << 20) // math.isqrt(grade ** slope) + 1 for grade in range(2, number_of + 1)]
    spare, given = total - reach - (number_of - 1), [1] * (number_of - 1)
    while spare > 0:
        movable = [i for i in range(number_of - 1) if given[i] < reach]
        mass, budget = sum([weights[i] for i in movable]), spare
        for i in movable:
            more = min(reach - given[i], max(1, budget * weights[i] // mass), spare)
            given[i] = given[i] + more
            spare = spare - more
    return np.array([reach] + given)


def ragged_sizes(stream_key, number_of, total, most, slope):
    if number_of == 2:
        one = jax.random.randint(stream_key, (), max(1, total - most), min(most, total - 1) + 1)
        return jnp.stack([one, total - one])
    tallies = jnp.asarray(split_up(number_of, total, most, slope), jnp.int32)
    twos = (number_of - 1) // 2
    source_of, sink = tallies[1:1 + 2 * twos:2], tallies[2:2 + 2 * twos:2]
    room = jnp.minimum(source_of - 1, most - sink)
    shifted = jax.random.randint(jax.random.fold_in(stream_key, 1), (twos,), 0, 1 << 20) % (room + 1)
    tallies = tallies.at[1:1 + 2 * twos:2].set(source_of - shifted).at[2:2 + 2 * twos:2].set(sink + shifted)
    return tallies[jax.random.permutation(jax.random.fold_in(stream_key, 2), number_of)]


def assign_block(own_key, own, number, rows, count, top, most, lean):
    order = jax.random.permutation(own_key, count)
    crowded, usual = load_shares(count, rows * top, most, lean, True), load_shares(count, rows * top, most, lean, False)
    places = jnp.arange(count)

    def named(lengths, rotation):
        used = int((lengths > 0).sum())
        fixed = max(1, used // 4)
        shifted = fixed + (places - fixed + rotation * (used - fixed)) % max(1, count - fixed)
        return jnp.zeros((count,), jnp.int32).at[order[jnp.where(places < fixed, places, shifted)]].set(jnp.asarray(lengths, jnp.int32))

    lengths = jnp.where(number % 4 == 0, named(crowded, number // 4), named(usual, number - number // 4 - 1))
    mixed = jax.random.permutation(jax.random.fold_in(own, 3), count)
    giver, taker = mixed[0:count // 2 * 2:2], mixed[1:count // 2 * 2:2]
    slack = jnp.minimum(lengths[giver] - 1, most - lengths[taker]) // 2
    slack = jnp.where((giver == order[0]) | (taker == order[0]) | (lengths[taker] == 0), 0, jnp.maximum(slack, 0))
    shifted = jax.random.randint(jax.random.fold_in(own, 4), (count // 2,), 0, 1 << 20) % (slack + 1)
    lengths = lengths.at[giver].add(-shifted).at[taker].add(shifted)
    labels = jnp.searchsorted(jnp.cumsum(lengths), jnp.arange(rows * top), side="right").astype(jnp.int32)
    grid = labels.reshape(top, rows).T
    grid = grid[jax.random.permutation(jax.random.fold_in(own, 1), rows)]
    rotation = jax.random.randint(jax.random.fold_in(own, 2), (rows, 1), 0, top)
    return jnp.take_along_axis(grid, (jnp.arange(top)[None, :] + rotation) % top, axis=1)


def load_shares(amount, total, limit, lean, full):
    portions = [(1 << 20) // math.isqrt(standing ** lean) + 1 for standing in range(1, amount + 1)]
    largest = limit if full else min(limit, max(-(-total // amount), total * portions[0] // sum(portions)))
    least = 1 if total - largest >= amount - 1 else 0
    holding, spare = [largest] + [least] * (amount - 1), total - largest - least * (amount - 1)
    while spare > 0:
        movable = [i for i in range(1, amount) if holding[i] < largest] or [i for i in range(1, amount) if holding[i] < limit]
        whole, remaining = sum([portions[i] for i in movable]), spare
        for i in movable:
            more = min(limit - holding[i], max(1, remaining * portions[i] // whole), spare)
            holding[i] = holding[i] + more
            spare = spare - more
    return np.array(holding)


def bell_draw(rng, extent, deviation, limit, split=(), kind=jnp.bfloat16):
    drawn = jax.random.normal(rng, extent, jnp.float32) * deviation
    if len(split) > 0:
        drawn = shard_levels(rng, extent, split, -0.22, 0.18) * drawn
    return jnp.clip(drawn, min=-limit, max=limit).astype(kind)


def setup_inputs(seed: int = 0) -> dict:
    streams_of = jax.random.split(jax.random.key(seed), 13)
    q_nope = bell_draw(streams_of[0], (ATT_ROWS, HEADS * NOPE), 1.0, 6.0, ((0, 32), (1, 4)))
    q_rope = draw_q_rope(jax.random.fold_in(streams_of[12], 71), 0)
    kv_latent = draw_kv_latent(jax.random.fold_in(streams_of[12], 71), 0)
    group_ids = jnp.searchsorted(jnp.cumsum(ragged_sizes(streams_of[3], GROUPS, ATT_ROWS, ATT_TOK, 1)), jnp.arange(ATT_ROWS), side="right").astype(jnp.int32)
    w_uk = bell_draw(streams_of[4], (HEADS, NOPE, LAT), NOPE ** -0.5, 0.5, ((0, 4),))
    w_uv = bell_draw(streams_of[5], (HEADS, LAT, VDIM), LAT ** -0.5, 0.25, ((0, 4),))
    moe_in = bell_draw(streams_of[6], (MOE_ROWS, D), 1.0, 6.0, ((0, 32), (1, 4)))
    expert_ids_keys = jax.random.split(jax.random.fold_in(streams_of[7], 1), MOE_ROWS // MOE_TOK)
    expert_ids_turns = jax.random.permutation(jax.random.fold_in(streams_of[7], 3), MOE_ROWS // MOE_TOK)
    expert_ids = jax.vmap(lambda own, number: assign_block(jax.random.fold_in(streams_of[7], 2), own, number, MOE_TOK, EXPERTS, TOPW, CAP, 2))(expert_ids_keys, expert_ids_turns).reshape((MOE_ROWS, TOPW))
    gate_w = jnp.clip(jnp.exp(math.log(1.0) - 2.3025851 * jax.random.uniform(streams_of[8], (MOE_ROWS, TOPW), jnp.float32) ** shard_levels(streams_of[8], (MOE_ROWS, TOPW), ((0, 32),), -0.2, 0.2)), 0.1, 1.0)
    w_gate = bell_draw(streams_of[9], (EXPERTS, D, FF), D ** -0.5, 0.0625, ((0, 32), (1, 4)))
    w_up = bell_draw(streams_of[10], (EXPERTS, D, FF), D ** -0.5, 0.0625, ((0, 32), (1, 4)))
    w_down = bell_draw(streams_of[11], (EXPERTS, FF, D), FF ** -0.5, 0.1875, ((0, 32), (2, 4)))
    return dict(q_nope=q_nope, q_rope=q_rope, kv_latent=kv_latent, group_ids=group_ids, w_uk=w_uk, w_uv=w_uv, moe_in=moe_in, expert_ids=expert_ids, gate_w=gate_w, w_gate=w_gate, w_up=w_up, w_down=w_down)


def attend_block(query_nope, query_rope, key_block, key_ids, query_ids, w_uk, w_uv):
    tok_count = query_nope.shape[0]
    head_count = w_uk.shape[0]
    nope_width = w_uk.shape[1]
    lat_width = w_uk.shape[2]
    rope_width = query_rope.shape[1] // head_count
    q_split = query_nope.reshape(tok_count, head_count, nope_width).astype(jnp.float32)
    r_split = query_rope.reshape(tok_count, head_count, rope_width).astype(jnp.float32)
    q_latent = jnp.einsum("thn,hnl->htl", q_split, w_uk.astype(jnp.float32)).astype(jnp.bfloat16)
    q_latent = lax.optimization_barrier(q_latent)
    latent = key_block[:, :lat_width].astype(jnp.float32)
    rotary = key_block[:, lat_width:].astype(jnp.float32)
    scale_factor = (nope_width + rope_width) ** -0.5
    scores = jnp.einsum("htl,kl->htk", q_latent.astype(jnp.float32), latent)
    scores = (scores + jnp.einsum("thr,kr->htk", r_split, rotary)) * scale_factor
    key_count = key_block.shape[0]
    query_pos = jnp.arange(tok_count, dtype=jnp.int32) + (key_count - tok_count)
    key_pos = jnp.arange(key_count, dtype=jnp.int32)
    allowed = (key_ids[None, :] == query_ids[:, None]) & (key_pos[None, :] <= query_pos[:, None])
    scores = jnp.where(allowed[None], scores, -jnp.inf)
    highest = jnp.max(scores, axis=2, keepdims=True)
    expo = jnp.exp(scores - highest)
    probs = (expo / jnp.sum(expo, axis=2, keepdims=True)).astype(jnp.bfloat16)
    probs = lax.optimization_barrier(probs)
    mixed_latent = jnp.einsum("htk,kl->htl", probs.astype(jnp.float32), latent).astype(jnp.bfloat16)
    mixed_latent = lax.optimization_barrier(mixed_latent)
    heads_out = jnp.einsum("htl,hlv->thv", mixed_latent.astype(jnp.float32), w_uv.astype(jnp.float32))
    return heads_out.astype(jnp.bfloat16).reshape(tok_count, head_count * w_uv.shape[2])


def reference(q_nope, q_rope, kv_latent, group_ids, w_uk, w_uv, moe_in, expert_ids, gate_w, w_gate, w_up, w_down):
    padded_kv = jnp.concatenate([jnp.zeros((ATT_TOK, LAT + ROPE), jnp.bfloat16), kv_latent], axis=0)
    padded_ids = jnp.concatenate([jnp.full((ATT_TOK,), -1, jnp.int32), group_ids.astype(jnp.int32)])
    query_blocks = q_nope.reshape(N_SEQ, ATT_TOK, HEADS * NOPE)
    rope_blocks = q_rope.reshape(N_SEQ, ATT_TOK, HEADS * ROPE)

    def one_block(inputs):
        block_idx, query_nope, query_rope = inputs
        start = (block_idx * ATT_TOK).astype(jnp.int32)
        key_block = lax.dynamic_slice_in_dim(padded_kv, start, 2 * ATT_TOK, 0)
        key_ids = lax.dynamic_slice_in_dim(padded_ids, start, 2 * ATT_TOK, 0)
        query_ids = lax.dynamic_slice_in_dim(group_ids.astype(jnp.int32), start, ATT_TOK, 0)
        return attend_block(query_nope, query_rope, key_block, key_ids, query_ids, w_uk, w_uv)

    attn_blocks = lax.map(one_block, (jnp.arange(N_SEQ, dtype=jnp.int32), query_blocks, rope_blocks))
    attn_out = attn_blocks.reshape(ATT_ROWS, HEADS * VDIM)

    flat_ids = expert_ids.astype(jnp.int32).reshape(N_SEQ, MOE_TOK * TOPW)
    onehot = (flat_ids[..., None] == jnp.arange(EXPERTS, dtype=jnp.int32)).astype(jnp.int32)
    before = jnp.cumsum(onehot, axis=1) - onehot
    slot_of = jnp.sum(before * onehot, axis=2).reshape(MOE_ROWS, TOPW)
    block_of = jnp.broadcast_to((jnp.arange(MOE_ROWS, dtype=jnp.int32) // MOE_TOK)[:, None], (MOE_ROWS, TOPW))
    pair_ids = jnp.arange(MOE_ROWS * TOPW, dtype=jnp.int32).reshape(MOE_ROWS, TOPW)
    table = jnp.full((EXPERTS, N_SEQ, CAP), MOE_ROWS * TOPW, jnp.int32)
    table = table.at[expert_ids.astype(jnp.int32), block_of, slot_of].set(pair_ids)
    padded_in = jnp.concatenate([moe_in, jnp.zeros((1, D), jnp.bfloat16)], axis=0)
    padded_gate = jnp.concatenate([gate_w.reshape(-1), jnp.zeros((1,), jnp.float32)])

    def one_expert(accum, inputs):
        slot_pairs, gate_mat, up_mat, down_mat = inputs
        token_idx = slot_pairs // TOPW
        chosen = padded_in[token_idx]
        gate_pre = jnp.dot(chosen, gate_mat, preferred_element_type=jnp.float32)
        up_pre = jnp.dot(chosen, up_mat, preferred_element_type=jnp.float32)
        hidden = (jax.nn.silu(gate_pre) * up_pre).astype(jnp.bfloat16)
        expert_out = jnp.dot(hidden, down_mat, preferred_element_type=jnp.float32).astype(jnp.bfloat16)
        expert_out = lax.optimization_barrier(expert_out)
        weight = padded_gate[slot_pairs]
        accum = accum.at[token_idx].add(weight[:, None] * expert_out.astype(jnp.float32))
        return accum, None

    start_acc = jnp.zeros((MOE_ROWS + 1, D), jnp.float32)
    accum, _ = lax.scan(one_expert, start_acc, (table.reshape(EXPERTS, N_SEQ * CAP), w_gate, w_up, w_down))
    moe_out = (moe_in.astype(jnp.float32) + accum[:MOE_ROWS]).astype(jnp.bfloat16)
    return attn_out, moe_out
```

```python
import functools
import jax
import jax.numpy as jnp
from jax import lax
from jax.experimental import pallas as pl
from jax.experimental.pallas import tpu as pltpu
from jax.sharding import PartitionSpec as P

SLOT_SPLIT = (16, 16)
ATT_CALLS = 2
HEADS_STEP = 4
BF, F32, I32 = jnp.bfloat16, jnp.float32, jnp.int32


def rank_of_routes(ids):
    experts, tokens = 32, ids.shape[1]
    expert = lax.broadcasted_iota(I32, (experts, tokens), 0)
    named = (ids[0:1, :] == expert) | (ids[1:2, :] == expert)
    row = lax.broadcasted_iota(I32, (tokens, tokens), 0)
    col = lax.broadcasted_iota(I32, (tokens, tokens), 1)
    before = jnp.where(row < col, 1.0, 0.0).astype(BF)
    count = jnp.dot(jnp.where(named, 1.0, 0.0).astype(BF), before, preferred_element_type=F32)
    return jnp.where(named, count.astype(I32), -1)


def dispatch_kernel(first, slots, ids_ref, tokens_ref, out_ref, pick_ref):
    @pl.when(pl.program_id(0) == 0)
    def _():
        rank = rank_of_routes(ids_ref[...])
        experts, tokens = rank.shape
        slot = lax.broadcasted_iota(I32, (experts, slots, tokens), 1) + first
        pick = jnp.where(rank[:, None, :] == slot, 1.0, 0.0)
        pick_ref[...] = pick.reshape(experts * slots, tokens).astype(BF)

    out_ref[...] = jnp.dot(pick_ref[...], tokens_ref[...], preferred_element_type=F32).astype(BF)


def dispatch(ids, tokens, first, slots):
    count, width = tokens.shape
    rows, step = 32 * slots, 896
    return pl.pallas_call(
        functools.partial(dispatch_kernel, first, slots),
        out_shape=jax.ShapeDtypeStruct((rows, width), BF),
        grid=(width // step,),
        in_specs=[
            pl.BlockSpec((2, count), lambda j: (0, 0)),
            pl.BlockSpec((count, step), lambda j: (0, j)),
        ],
        out_specs=pl.BlockSpec((rows, step), lambda j: (0, j)),
        scratch_shapes=[pltpu.VMEM((rows, count), BF)],
        cost_estimate=pl.CostEstimate(
            flops=2 * rows * count * width, bytes_accessed=2 * (rows + count) * width, transcendentals=0
        ),
        name="dispatch",
    )(ids, tokens)


def gate_up_kernel(quarter, me_ref, rows_ref, gate_ref, up_ref, own_ref, out1, out2, out3, ordered):
    step = gate_ref.shape[1]

    @pl.when(pl.program_id(0) == 0)
    def _():
        for shift in range(4):
            there = lax.rem(me_ref[0] + shift, 4)
            source = pl.ds(pl.multiple_of(there * quarter, quarter), quarter)
            ordered[shift * quarter : (shift + 1) * quarter, :] = rows_ref[source, :]

    for at, weight in ((0, gate_ref), (step, up_ref)):
        total = jnp.dot(ordered[...], weight[...], preferred_element_type=F32)
        own_ref[:, at : at + step] = total[:quarter, :]
        for shift, out in ((1, out1), (2, out2), (3, out3)):
            out[:, at : at + step] = total[shift * quarter : (shift + 1) * quarter, :].astype(BF)


def gate_up(me, rows, gate, up):
    count, depth = rows.shape
    width, step = gate.shape[1], 256
    quarter = count // 4
    block = pl.BlockSpec((quarter, 2 * step), lambda j: (0, j))
    sent = jax.ShapeDtypeStruct((quarter, 2 * width), BF)
    return pl.pallas_call(
        functools.partial(gate_up_kernel, quarter),
        out_shape=(jax.ShapeDtypeStruct((quarter, 2 * width), F32), sent, sent, sent),
        grid=(width // step,),
        in_specs=[
            pl.BlockSpec(memory_space=pltpu.SMEM),
            pl.BlockSpec((count, depth), lambda j: (0, 0)),
            pl.BlockSpec((depth, step), lambda j: (0, j)),
            pl.BlockSpec((depth, step), lambda j: (0, j)),
        ],
        out_specs=(block, block, block, block),
        scratch_shapes=[pltpu.VMEM((count, depth), BF)],
        cost_estimate=pl.CostEstimate(
            flops=4 * count * depth * width, bytes_accessed=4 * depth * width, transcendentals=0
        ),
        name="gate_up",
    )(me, rows, gate, up)


def hidden_kernel(own_ref, got1, got2, got3, out_ref):
    step = 256
    for j in range(out_ref.shape[1] // step):
        both = slice(2 * j * step, 2 * (j + 1) * step)
        total = own_ref[:, both] + got1[:, both].astype(F32)
        total = total + got2[:, both].astype(F32) + got3[:, both].astype(F32)
        gate, up = total[:, :step], total[:, step:]
        out_ref[:, j * step : (j + 1) * step] = (gate / (1.0 + jnp.exp(-gate)) * up).astype(BF)


def hidden_of(own, got):
    quarter, twice = own.shape
    return pl.pallas_call(
        hidden_kernel,
        out_shape=jax.ShapeDtypeStruct((quarter, twice // 2), BF),
        in_specs=[pl.BlockSpec(memory_space=pltpu.VMEM)] * 4,
        out_specs=pl.BlockSpec(memory_space=pltpu.VMEM),
        cost_estimate=pl.CostEstimate(
            flops=8 * quarter * twice, bytes_accessed=10 * quarter * twice, transcendentals=quarter * twice // 2
        ),
        name="hidden",
    )(own, *got)


def down_kernel(quarter, me_ref, own_ref, got1, got2, got3, down_ref, out_ref, joined):
    @pl.when(pl.program_id(0) == 0)
    def _():
        me = me_ref[0]
        for shift, piece in ((0, own_ref), (1, got1), (2, got2), (3, got3)):
            origin = lax.rem(me + 4 - shift, 4)
            joined[pl.ds(pl.multiple_of(origin * quarter, quarter), quarter), :] = piece[...]

    out_ref[...] = jnp.dot(joined[...], down_ref[...], preferred_element_type=F32).astype(BF)


def down_of(me, own, got, down):
    quarter, depth = own.shape
    width, step = down.shape[1], 896
    whole = pl.BlockSpec((quarter, depth), lambda j: (0, 0))
    return pl.pallas_call(
        functools.partial(down_kernel, quarter),
        out_shape=jax.ShapeDtypeStruct((4 * quarter, width), BF),
        grid=(width // step,),
        in_specs=[pl.BlockSpec(memory_space=pltpu.SMEM)]
        + [whole] * 4
        + [pl.BlockSpec((depth, step), lambda j: (0, j))],
        out_specs=pl.BlockSpec((4 * quarter, step), lambda j: (0, j)),
        scratch_shapes=[pltpu.VMEM((4 * quarter, depth), BF)],
        cost_estimate=pl.CostEstimate(
            flops=8 * quarter * depth * width, bytes_accessed=2 * depth * width, transcendentals=0
        ),
        name="down",
    )(me, own, *got, down)


def tables_kernel(split, ids_ref, weight_ref, *outs):
    tokens = ids_ref.shape[1]
    ids, weight = ids_ref[...], weight_ref[...]
    rank = rank_of_routes(ids)
    experts = rank.shape[0]
    expert = lax.broadcasted_iota(I32, (experts, tokens), 0)
    value = jnp.where(ids[0:1, :] == expert, weight[0:1, :], 0.0)
    value = value + jnp.where(ids[1:2, :] == expert, weight[1:2, :], 0.0)
    first = 0
    for slots, out in zip(split, outs):
        slot = lax.broadcasted_iota(I32, (experts, slots, tokens), 1) + first
        table = jnp.where(rank[:, None, :] == slot, value[:, None, :], 0.0)
        table = table.reshape(experts * slots, tokens).T
        high = table.astype(BF)
        out[:tokens, :] = high
        out[tokens:, :] = (table - high.astype(F32)).astype(BF)
        first += slots


def tables(ids, weight, split):
    tokens = ids.shape[1]
    return pl.pallas_call(
        functools.partial(tables_kernel, split),
        out_shape=tuple(jax.ShapeDtypeStruct((2 * tokens, 32 * slots), BF) for slots in split),
        cost_estimate=pl.CostEstimate(flops=10**7, bytes_accessed=4 * tokens * 32 * sum(split), transcendentals=0),
        name="tables",
    )(ids, weight)


def combine_kernel(table_ref, back_ref, base_ref, out_ref):
    tokens = base_ref.shape[0]
    both = jnp.dot(table_ref[...], back_ref[...], preferred_element_type=F32)
    total = base_ref[...].astype(F32) + both[:tokens, :] + both[tokens:, :]
    out_ref[...] = total.astype(out_ref.dtype)


def combine(table, back, base, kind):
    tokens = base.shape[0]
    rows, width = back.shape
    step = 896
    return pl.pallas_call(
        combine_kernel,
        out_shape=jax.ShapeDtypeStruct((tokens, width), kind),
        grid=(width // step,),
        in_specs=[
            pl.BlockSpec((2 * tokens, rows), lambda j: (0, 0)),
            pl.BlockSpec((rows, step), lambda j: (0, j)),
            pl.BlockSpec((tokens, step), lambda j: (0, j)),
        ],
        out_specs=pl.BlockSpec((tokens, step), lambda j: (0, j)),
        cost_estimate=pl.CostEstimate(
            flops=4 * tokens * rows * width, bytes_accessed=2 * (rows + 3 * tokens) * width, transcendentals=0
        ),
        name="combine",
    )(table, back, base)


def attend_kernel(scale, me_ref, ids_ref, before_ref, here_ref, nope_ref, rope_ref, uk_ref, uv_ref, *rest):
    out_ref, keys, values, bias, queries, mixed = rest[-6:]
    tokens = nope_ref.shape[0]
    latent = uk_ref.shape[2]
    heads = uk_ref.shape[0]
    rotary = here_ref.shape[0] - latent

    @pl.when(pl.program_id(0) == 0)
    def _():
        for at, part in ((0, before_ref), (tokens, here_ref)):
            keys[: latent + rotary, at : at + tokens] = part[...]
            keys[latent + rotary :, at : at + tokens] = part[latent:, :]
            values[at : at + tokens, :] = part[:latent, :].astype(F32).T.astype(BF)
        me = me_ref[0]
        own = ids_ref[pl.ds(me, 1), :]
        prior = ids_ref[pl.ds(jnp.maximum(me - 1, 0), 1), :]
        prior = jnp.where(me == 0, -1, prior)
        row = lax.broadcasted_iota(I32, (tokens, tokens), 0)
        col = lax.broadcasted_iota(I32, (tokens, tokens), 1)
        mine = jnp.sum(jnp.where(row == col, own, 0), axis=1, keepdims=True)
        bias[:, :tokens] = jnp.where(mine == prior, 0.0, -1e30)
        bias[:, tokens:] = jnp.where((mine == own) & (col <= row), 0.0, -1e30)

    lane = lax.broadcasted_iota(I32, (tokens, 2 * rotary), 1)
    for h in range(heads):
        rows = slice(h * tokens, (h + 1) * tokens)
        nope = nope_ref[:, h * 128 : (h + 1) * 128]
        queries[rows, :latent] = jnp.dot(nope, uk_ref[h], preferred_element_type=F32).astype(BF)
        pair = rope_ref[:, (h // 2) * 2 * rotary : (h // 2 + 1) * 2 * rotary]
        inside = (lane < rotary) if h % 2 == 0 else (lane >= rotary)
        queries[rows, latent:] = jnp.where(inside, pair.astype(F32), 0.0).astype(BF)
    scores = jnp.dot(queries[...], keys[...], preferred_element_type=F32) * scale
    scores = scores.reshape(heads, tokens, 2 * tokens) + bias[...][None]
    scores = scores.reshape(heads * tokens, 2 * tokens)
    expo = jnp.exp(scores - jnp.max(scores, axis=1, keepdims=True))
    probs = (expo / jnp.sum(expo, axis=1, keepdims=True)).astype(BF)
    mixed[...] = jnp.dot(probs, values[...], preferred_element_type=F32).astype(BF)
    for h in range(heads):
        rows = slice(h * tokens, (h + 1) * tokens)
        out = jnp.dot(mixed[rows, :], uv_ref[h], preferred_element_type=F32)
        out_ref[:, h * 128 : (h + 1) * 128] = out.astype(BF)


def attend(me, ids, before, here, nope, rope, uk, uv, part, parts, so_far):
    tokens = nope.shape[0]
    heads, _, latent = uk.shape
    rotary = here.shape[0] - latent
    step = HEADS_STEP
    steps = heads // step // parts
    base = part * steps
    scale = (128 + rotary) ** (-0.5)
    whole = lambda a: pl.BlockSpec(a.shape, lambda j: (0, 0))
    in_specs = [
        pl.BlockSpec(memory_space=pltpu.SMEM),
        whole(ids),
        whole(before),
        whole(here),
        pl.BlockSpec((tokens, step * 128), lambda j: (0, base + j)),
        pl.BlockSpec((tokens, step * rotary), lambda j: (0, base + j)),
        pl.BlockSpec((step, 128, latent), lambda j: (base + j, 0, 0)),
        pl.BlockSpec((step, latent, 128), lambda j: (base + j, 0, 0)),
    ]
    args = [me, ids, before, here, nope, rope, uk, uv]
    aliases = {}
    if so_far is not None:
        in_specs.append(pl.BlockSpec(memory_space=pl.ANY))
        aliases = {len(args): 0}
        args.append(so_far)
    return pl.pallas_call(
        functools.partial(attend_kernel, scale),
        out_shape=jax.ShapeDtypeStruct((tokens, heads * 128), BF),
        grid=(steps,),
        in_specs=in_specs,
        out_specs=pl.BlockSpec((tokens, step * 128), lambda j: (0, base + j)),
        scratch_shapes=[
            pltpu.VMEM((latent + 2 * rotary, 2 * tokens), BF),
            pltpu.VMEM((2 * tokens, latent), BF),
            pltpu.VMEM((tokens, 2 * tokens), F32),
            pltpu.VMEM((step * tokens, latent + 2 * rotary), BF),
            pltpu.VMEM((step * tokens, latent), BF),
        ],
        input_output_aliases=aliases,
        cost_estimate=pl.CostEstimate(
            flops=heads // parts * tokens * 2 * (2 * 128 * latent + 2 * tokens * (2 * latent + 2 * rotary)),
            bytes_accessed=heads // parts * 128 * latent * 4,
            transcendentals=heads // parts * tokens * tokens * 2,
        ),
        name="attend",
    )(*args)


def shifted(value, axis, shift):
    count = lax.axis_size(axis)
    return lax.ppermute(value, axis, [(i, (i + shift) % count) for i in range(count)])


def on_device(
    q_nope, q_rope, kv_latent, group_ids, w_uk, w_uv, moe_in, expert_ids, gate_w, w_gate, w_up, w_down
):
    seq, head = lax.axis_index("seq"), lax.axis_index("head")
    me_seq, me_head = seq.reshape(1).astype(I32), head.reshape(1).astype(I32)
    ids, weight = expert_ids.T, gate_w.T
    width = moe_in.shape[1]

    def exchange(value, slots):
        value = value.reshape(32, slots, width)
        value = lax.all_to_all(value, "seq", split_axis=0, concat_axis=0, tiled=True)
        return value.reshape(32 * slots, width)

    here = kv_latent.T
    before = lax.ppermute(here, "seq", [(i, i + 1) for i in range(31)])
    arrived, first = [], 0
    for slots in SLOT_SPLIT:
        outgoing = dispatch(ids, moe_in, first, slots)
        arrived.append(exchange(outgoing, slots))
        first += slots
    table = tables(ids, weight, SLOT_SPLIT)
    group_rows = group_ids.reshape(32, -1)
    attn = None
    for part in range(ATT_CALLS):
        attn = attend(me_seq, group_rows, before, here, q_nope, q_rope, w_uk, w_uv, part, ATT_CALLS, attn)

    total = moe_in
    for i, slots in enumerate(SLOT_SPLIT):
        own, *parts = gate_up(me_head, arrived[i], w_gate[0], w_up[0])
        got = []
        for s in (1, 2, 3):
            got.append(shifted(parts[s - 1], "head", s))
        hidden = hidden_of(own, got)
        got = []
        for s in (1, 2, 3):
            got.append(shifted(hidden, "head", s))
        result = down_of(me_head, hidden, got, w_down[0])
        back = exchange(result, slots)
        total = combine(table[i], back, total, BF if i == len(SLOT_SPLIT) - 1 else F32)
    return attn, total


def solution(mesh):
    return jax.shard_map(
        on_device,
        mesh=mesh,
        in_specs=(
            P("seq", "head"),
            P("seq", "head"),
            P("seq", None),
            P(),
            P("head", None, None),
            P("head", None, None),
            P("seq", "head"),
            P("seq", None),
            P("seq", None),
            P("seq", "head", None),
            P("seq", "head", None),
            P("seq", None, "head"),
        ),
        out_specs=(P("seq", "head"), P("seq", "head")),
        check_vma=False,
    )
```
